32 devices in a mesh: dp: 2 (over y), ctx: 4 (over x, core), exp: 4 (over z).
Axes of the slice: x: 2, y: 2, z: 4, core: 2. Of those that a mesh axis runs over, the one named last changes fastest.
Arguments:
- tokens: bfloat16 [4096, 2048], P(('dp', 'ctx', 'exp')), may hold values from -6 to 6
- cotangent: bfloat16 [4096, 2048], P(('dp', 'ctx', 'exp')), may hold values from -6 to 6
- expert_ids: int32 [4096, 1], P(('dp', 'ctx', 'exp')), may hold values from 0 to 7; in each aligned block of 128 rows (0 to 127, 128 to 255, ...) at most 24 rows name the same one
- router_weight: bfloat16 [2048, 8], replicated, may hold values from -0.125 to 0.125
- gate_up: bfloat16 [8, 2048, 1408], P(('dp', 'exp')), may hold values from -0.125 to 0.125
- down_weight: bfloat16 [8, 704, 2048], P(('dp', 'exp')), may hold values from -0.21875 to 0.21875
Outputs:
- moe_out: bfloat16 [4096, 2048], P(('dp', 'ctx', 'exp'))
- token_grad: bfloat16 [4096, 2048], P(('dp', 'ctx', 'exp'))
- router_grad: float32 [2048, 8], replicated
The draws below stay inside these ranges and needn't reach their ends.
Inputs may be any that keep to these rules, and one draw needn't show every extreme that they name: `expert_ids`: each token names 1 different experts; among the 128 tokens of one device (aligned blocks of 128 rows) no expert is named more than 24 times, a bound that some block reaches.
All inputs are finite; a program needn't handle non-finite values.
Results may differ from the reference program's by a relative error of at most 0.0064.
Values may be sent and summed in bfloat16 or wider, within the bound.
A program may use at most 64 MiB of HBM per device.

```python
import math
import jax
import jax.numpy as jnp
import numpy as np
from jax import lax

D = 2048
FF = 704
TOP = 1
TOK_DEV = 128
EXPERTS = 8
CAP = 24
TOKENS = 4096
N_DP = 2
N_CTX = 4
N_EXP = 4


def levels(key, extent, pieces, least, high):
    loudness = 1.0
    for dim, shards_of in pieces:
        draws = jax.random.uniform(jax.random.fold_in(jax.random.fold_in(key, 6), dim), (shards_of,), jnp.float32, least / len(pieces), high / len(pieces))
        loudness = loudness * jnp.repeat(jnp.exp(draws), extent[dim] // shards_of).reshape((-1,) + (1,) * (len(extent) - 1 - dim))
    return loudness


def routed_block(own_key, own, number, rows, number_of, top, most, lean):
    ranking = jax.random.permutation(own_key, number_of)
    heavy_load, ordinary = shares(number_of, rows * top, most, lean, True), shares(number_of, rows * top, most, lean, False)
    places = jnp.arange(number_of)

    def named(lengths, turn):
        used = int((lengths > 0).sum())
        fixed = max(1, used // 4)
        shifted = fixed + (places - fixed + turn * (used - fixed)) % max(1, number_of - fixed)
        return jnp.zeros((number_of,), jnp.int32).at[ranking[jnp.where(places < fixed, places, shifted)]].set(jnp.asarray(lengths, jnp.int32))

    lengths = jnp.where(number % 4 == 0, named(heavy_load, number // 4), named(ordinary, number - number // 4 - 1))
    mixed = jax.random.permutation(jax.random.fold_in(own, 3), number_of)
    source_of, sink = mixed[0:number_of // 2 * 2:2], mixed[1:number_of // 2 * 2:2]
    slack = jnp.minimum(lengths[source_of] - 1, most - lengths[sink]) // 2
    slack = jnp.where((source_of == ranking[0]) | (sink == ranking[0]) | (lengths[sink] == 0), 0, jnp.maximum(slack, 0))
    shifted = jax.random.randint(jax.random.fold_in(own, 4), (number_of // 2,), 0, 1 << 20) % (slack + 1)
    lengths = lengths.at[source_of].add(-shifted).at[sink].add(shifted)
    members = jnp.searchsorted(jnp.cumsum(lengths), jnp.arange(rows * top), side="right").astype(jnp.int32)
    grid = members.reshape(top, rows).T
    grid = grid[jax.random.permutation(jax.random.fold_in(own, 1), rows)]
    turn = jax.random.randint(jax.random.fold_in(own, 2), (rows, 1), 0, top)
    return jnp.take_along_axis(grid, (jnp.arange(top)[None, :] + turn) % top, axis=1)


def shares(count, total, reach, slope, full):
    weights = [(1 << 20) // math.isqrt(standing ** slope) + 1 for standing in range(1, count + 1)]
    largest = reach if full else min(reach, max(-(-total // count), total * weights[0] // sum(weights)))
    least = 1 if total - largest >= count - 1 else 0
    counts, surplus = [largest] + [least] * (count - 1), total - largest - least * (count - 1)
    while surplus > 0:
        movable = [i for i in range(1, count) if counts[i] < largest] or [i for i in range(1, count) if counts[i] < reach]
        whole, left = sum([weights[i] for i in movable]), surplus
        for i in movable:
            extra = min(reach - counts[i], max(1, left * weights[i] // whole), surplus)
            counts[i] = counts[i] + extra
            surplus = surplus - extra
    return np.array(counts)


def normal_values(stream_key, extent, scale, reach, split=(), kind=jnp.bfloat16):
    array = jax.random.normal(stream_key, extent, jnp.float32) * scale
    if len(split) > 0:
        array = levels(stream_key, extent, split, -0.22, 0.18) * array
    return jnp.clip(array, min=-reach, max=reach).astype(kind)


def setup_inputs(seed: int = 0) -> dict:
    key_of = jax.random.split(jax.random.key(seed), 7)
    tokens = normal_values(key_of[0], (TOKENS, D), 1.0, 6.0, ((0, 32),))
    cotangent = normal_values(key_of[1], (TOKENS, D), 1.0, 6.0, ((0, 32),))
    expert_ids_keys = jax.random.split(jax.random.fold_in(key_of[2], 1), TOKENS // TOK_DEV)
    expert_ids_turns = jax.random.permutation(jax.random.fold_in(key_of[2], 3), TOKENS // TOK_DEV)
    expert_ids = jax.vmap(lambda own, number: routed_block(jax.random.fold_in(key_of[2], 2), own, number, TOK_DEV, EXPERTS, TOP, CAP, 2))(expert_ids_keys, expert_ids_turns).reshape((TOKENS, TOP))
    router_weight = normal_values(key_of[3], (D, EXPERTS), D ** -0.5, 0.125)
    gate_up = normal_values(key_of[4], (EXPERTS, D, 2 * FF), D ** -0.5, 0.125, ((0, 8),))
    down_weight = normal_values(key_of[5], (EXPERTS, FF, D), FF ** -0.5, 0.21875, ((0, 8),))
    return {"tokens": tokens, "cotangent": cotangent, "expert_ids": expert_ids, "router_weight": router_weight, "gate_up": gate_up, "down_weight": down_weight}


def expert_rows(inputs, upstream, w_in, w_out):
    hidden_units = w_out.shape[0]
    pre_act = jnp.dot(inputs, w_in, preferred_element_type=jnp.float32)
    gate_pre = pre_act[:, :hidden_units]
    up_pre = pre_act[:, hidden_units:]
    sig_gate = jax.nn.sigmoid(gate_pre)
    activated = gate_pre * sig_gate
    hidden = (activated * up_pre).astype(jnp.bfloat16)
    outputs = jnp.dot(hidden, w_out, preferred_element_type=jnp.float32).astype(jnp.bfloat16)
    back_hidden = lax.dot_general(upstream, w_out, (((1,), (1,)), ((), ())), preferred_element_type=jnp.float32)
    gate_slope = sig_gate * (1.0 + gate_pre * (1.0 - sig_gate))
    back_pre = jnp.concatenate([back_hidden * up_pre * gate_slope, back_hidden * activated], axis=1).astype(jnp.bfloat16)
    back_in = lax.dot_general(back_pre, w_in, (((1,), (1,)), ((), ())), preferred_element_type=jnp.float32).astype(jnp.bfloat16)
    return outputs, back_in


def reference(tokens, cotangent, expert_ids, router_weight, gate_up, down_weight):
    logits = jnp.dot(tokens, router_weight, preferred_element_type=jnp.float32)
    chosen = (expert_ids[:, :, None] == jnp.arange(EXPERTS, dtype=jnp.int32)[None, None, :]).astype(jnp.float32)
    picked = jnp.sum(chosen * logits[:, None, :], axis=2)
    gates = jax.nn.sigmoid(picked)
    flat_ids = expert_ids.reshape(-1)
    flat_gates = gates.reshape(-1)
    bound = N_DP * N_CTX * N_EXP * CAP

    def one_expert(carry, inputs_now):
        moe_acc, grad_acc, logit_acc = carry
        index, w_in, w_out = inputs_now
        member = flat_ids == index
        rows = jnp.nonzero(member, size=bound, fill_value=0)[0].astype(jnp.int32)
        count = jnp.sum(member.astype(jnp.int32))
        valid = (jnp.arange(bound, dtype=jnp.int32) < count).astype(jnp.float32)
        owner = (rows // TOP).astype(jnp.int32)
        row_inputs = tokens[owner]
        cot_rows = cotangent[owner].astype(jnp.float32)
        gate_rows = flat_gates[rows]
        upstream = (gate_rows[:, None] * cot_rows).astype(jnp.bfloat16)
        outputs, back_in = expert_rows(row_inputs, upstream, w_in, w_out)
        out_float = outputs.astype(jnp.float32)
        moe_acc = moe_acc.at[owner].add(valid[:, None] * gate_rows[:, None] * out_float)
        grad_acc = grad_acc.at[owner].add(valid[:, None] * back_in.astype(jnp.float32))
        agreement = jnp.sum(cot_rows * out_float, axis=1)
        logit_acc = logit_acc.at[rows].add(valid * gate_rows * (1.0 - gate_rows) * agreement)
        return (moe_acc, grad_acc, logit_acc), None

    start = (jnp.zeros(tokens.shape, jnp.float32), jnp.zeros(tokens.shape, jnp.float32), jnp.zeros(flat_ids.shape, jnp.float32))
    carry, unused = lax.scan(one_expert, start, (jnp.arange(EXPERTS, dtype=jnp.int32), gate_up, down_weight))
    moe_acc, grad_acc, logit_acc = carry
    moe_out = moe_acc.astype(jnp.bfloat16)
    logit_grad = logit_acc.reshape(gates.shape)
    dense_grad = jnp.sum(chosen * logit_grad[:, :, None], axis=1).astype(jnp.bfloat16)
    router_back = lax.dot_general(dense_grad, router_weight, (((1,), (1,)), ((), ())), preferred_element_type=jnp.float32)
    token_grad = (grad_acc + router_back).astype(jnp.bfloat16)
    router_grad = lax.dot_general(tokens, dense_grad, (((0,), (0,)), ((), ())), preferred_element_type=jnp.float32) / TOKENS
    return moe_out, token_grad, router_grad
```

```python
import functools

import jax
import jax.numpy as jnp
from jax import lax
from jax.experimental import pallas as pl
from jax.experimental.pallas import tpu as pltpu
from jax.sharding import PartitionSpec as P

MESH = pl.DeviceIdType.MESH
F32 = jnp.float32
BF16 = jnp.bfloat16
NT = (((1,), (1,)), ((), ()))


def plan(n_dp, n_exp):
    half = n_exp // 2
    cut = (half + 1) // 2
    far_a = [(d, 1, o) for o in range(cut) for d in range(n_dp)]
    near = [(d, 0, o) for o in range(half) for d in range(n_dp)]
    far_b = [(d, 1, o) for o in range(cut, half) for d in range(n_dp)]
    return [chunk for chunk in (far_a, near, far_b) if chunk]


def kernel(n_dp, n_ctx, n_exp, cap, total, tok, cot, ids, rw, gu_hbm, dn_hbm,
           moe_out, grad_out, rg_out,
           send, recv, res, ret, gu, dn, mine, summed, terms, columns,
           w_sem, fwd_send, fwd_recv, ret_send, ret_recv,
           ctx_send, ctx_recv, col_send, col_recv):
    me_dp, me_ctx, me_exp = lax.axis_index("dp"), lax.axis_index("ctx"), lax.axis_index("exp")
    me = me_dp * n_exp + me_exp
    half = n_exp // 2
    chunks = plan(n_dp, n_exp)
    slots = [slot for chunk in chunks for slot in chunk]
    count = len(slots)
    own = slots.index((0, 0, 0))
    tokens_here, width = tok.shape
    hidden_units = dn.shape[0]
    experts = rw.shape[1]
    rows = 2 * cap

    def peer(slot, way):
        d, h, o = slot
        if way < 0:
            d, h, o = (n_dp - d) % n_dp, h, (half - o) % half
        to_dp = lax.rem(me_dp + d, n_dp)
        to_half = lax.rem(me_exp // half + h, 2)
        to_low = lax.rem(lax.rem(me_exp, half) + o, half)
        return to_dp, to_half * half + to_low

    def at(pair):
        return {"dp": pair[0], "ctx": me_ctx, "exp": pair[1]}

    def at_ctx(j):
        return {"dp": me_dp, "ctx": j, "exp": me_exp}

    gu_copy = pltpu.make_async_copy(gu_hbm.at[0], gu, w_sem.at[0])
    dn_copy = pltpu.make_async_copy(dn_hbm.at[0], dn, w_sem.at[1])
    gu_copy.start()
    dn_copy.start()

    barrier = pltpu.get_barrier_semaphore()
    for k, slot in enumerate(slots):
        if k != own:
            pl.semaphore_signal(barrier, inc=1, device_id=at(peer(slot, 1)), device_id_type=MESH)
    for j in range(1, n_ctx):
        pl.semaphore_signal(
            barrier, inc=1, device_id=at_ctx(lax.rem(me_ctx + j, n_ctx)), device_id_type=MESH
        )

    ids_col = jnp.broadcast_to(ids[...], (tokens_here, tokens_here))
    r_iota = lax.broadcasted_iota(jnp.int32, (tokens_here, tokens_here), 0)
    c_iota = lax.broadcasted_iota(jnp.int32, (tokens_here, tokens_here), 1)
    ids_row = jnp.sum(jnp.where(r_iota == c_iota, ids_col, 0), axis=0, keepdims=True)
    same = ids_col == ids_row
    place_row = jnp.sum(jnp.where(same & (r_iota < c_iota), 1, 0), axis=0, keepdims=True)
    place_col = jnp.sum(jnp.where(same & (c_iota < r_iota), 1, 0), axis=1, keepdims=True)
    for k, slot in enumerate(slots):
        to_dp, to_exp = peer(slot, 1)
        expert = to_dp * n_exp + to_exp
        place_row = place_row + jnp.where(ids_row == expert, k * rows, 0)
        place_col = place_col + jnp.where(ids[...] == expert, k * rows, 0)

    pick_iota = lax.broadcasted_iota(jnp.int32, (count * rows, tokens_here), 0)
    pick_tok = jnp.where(pick_iota == place_row, 1.0, 0.0).astype(BF16)
    pick_cot = jnp.where(pick_iota == place_row + cap, 1.0, 0.0).astype(BF16)
    pick = jnp.concatenate([pick_tok, pick_cot], axis=1)
    stacked = jnp.concatenate([tok[...], cot[...]], axis=0)

    fwd = []
    back = []
    for k, slot in enumerate(slots):
        if k == own:
            fwd.append(None)
            back.append(None)
            continue
        fwd.append(
            pltpu.make_async_remote_copy(
                src_ref=send.at[k], dst_ref=recv.at[k],
                send_sem=fwd_send.at[k], recv_sem=fwd_recv.at[k],
                device_id=at(peer(slot, 1)), device_id_type=MESH,
            )
        )
        back.append(
            pltpu.make_async_remote_copy(
                src_ref=res.at[k], dst_ref=ret.at[k],
                send_sem=ret_send.at[k], recv_sem=ret_recv.at[k],
                device_id=at(peer(slot, -1)), device_id_type=MESH,
            )
        )

    first = 0
    for number, chunk in enumerate(chunks):
        last = first + len(chunk)
        packed = jnp.dot(
            pick[first * rows:last * rows], stacked, preferred_element_type=F32
        ).astype(BF16)
        send[first:last] = packed.reshape(len(chunk), rows, width)
        if number == 0:
            pl.semaphore_wait(barrier, count - 1 + n_ctx - 1)
        for k in range(first, last):
            if k != own:
                fwd[k].start()
        first = last

    lane_e = lax.broadcasted_iota(jnp.int32, (8, experts), 1)
    choose = jnp.where(lane_e == me, 1.0, 0.0).astype(BF16)
    router_row = lax.dot_general(choose, rw[...], NT, preferred_element_type=F32)[:1]

    gu_copy.wait()
    dn_copy.wait()

    router_sum = jnp.zeros((1, width), F32)
    first = 0
    for chunk in chunks:
        last = first + len(chunk)
        xs, cs = [], []
        for k in range(first, last):
            if k == own:
                block = send[k].astype(F32)
            else:
                fwd[k].wait_recv()
                block = recv[k].astype(F32)
            xs.append(block[:cap])
            cs.append(block[cap:])
        x_wide = jnp.concatenate(xs, axis=0)
        c_wide = jnp.concatenate(cs, axis=0)
        m = x_wide.shape[0]
        x = x_wide.astype(BF16)
        logits = jnp.dot(x, rw[...], preferred_element_type=F32)
        lane = lax.broadcasted_iota(jnp.int32, (m, experts), 1)
        gate = jax.nn.sigmoid(jnp.sum(jnp.where(lane == me, logits, 0.0), axis=1, keepdims=True))
        upstream = (gate * c_wide).astype(BF16)
        pre = jnp.dot(x, gu[...], preferred_element_type=F32)
        a = pre[:, :hidden_units]
        u = pre[:, hidden_units:]
        s = jax.nn.sigmoid(a)
        act = a * s
        hidden = (act * u).astype(BF16)
        out = jnp.dot(hidden, dn[...], preferred_element_type=F32).astype(BF16).astype(F32)
        back_hidden = lax.dot_general(upstream, dn[...], NT, preferred_element_type=F32)
        back_pre = jnp.concatenate(
            [back_hidden * u * (s * (1.0 + a * (1.0 - s))), back_hidden * act], axis=1
        ).astype(BF16)
        back_in = lax.dot_general(back_pre, gu[...], NT, preferred_element_type=F32)
        agreement = jnp.sum(c_wide * out, axis=1, keepdims=True)
        dense = (gate * (1.0 - gate) * agreement).astype(BF16).astype(F32)
        moe = gate * out
        grad = back_in.astype(BF16).astype(F32) + dense * router_row
        for i, k in enumerate(range(first, last)):
            part = slice(i * cap, (i + 1) * cap)
            block = jnp.concatenate([moe[part], grad[part]], axis=0).astype(BF16)
            if k == own:
                ret[k] = block
            else:
                res[k] = block
                back[k].start()
        router_sum = router_sum + jnp.sum(dense * x_wide, axis=0, keepdims=True)
        first = last

    router_sum = router_sum * (1.0 / total)
    lanes = width // mine.shape[0]
    for i in range(mine.shape[0]):
        mine[i:i + 1, :] = router_sum[:, i * lanes:(i + 1) * lanes]
    terms[me_ctx] = mine[...]
    ctx_copies = []
    for j in range(1, n_ctx):
        copy = pltpu.make_async_remote_copy(
            src_ref=mine, dst_ref=terms.at[me_ctx],
            send_sem=ctx_send.at[j], recv_sem=ctx_recv.at[me_ctx],
            device_id=at_ctx(lax.rem(me_ctx + j, n_ctx)), device_id_type=MESH,
        )
        copy.start()
        ctx_copies.append(copy)
    for j in range(1, n_ctx):
        source = lax.rem(me_ctx + j, n_ctx)
        pltpu.make_async_remote_copy(
            src_ref=mine, dst_ref=terms.at[source],
            send_sem=ctx_send.at[j], recv_sem=ctx_recv.at[source],
            device_id=at_ctx(source), device_id_type=MESH,
        ).wait_recv()
    column = terms[0]
    for j in range(1, n_ctx):
        column = column + terms[j]
    summed[...] = column
    columns[me] = column
    col_copies = []
    for k, slot in enumerate(slots):
        if k != own:
            copy = pltpu.make_async_remote_copy(
                src_ref=summed, dst_ref=columns.at[me],
                send_sem=col_send.at[k], recv_sem=col_recv.at[me],
                device_id=at(peer(slot, 1)), device_id_type=MESH,
            )
            copy.start()
            col_copies.append(copy)

    spot_iota = lax.broadcasted_iota(jnp.int32, (tokens_here, count * rows), 1)
    put_moe = jnp.where(spot_iota == place_col, 1.0, 0.0).astype(BF16)
    put_grad = jnp.where(spot_iota == place_col + cap, 1.0, 0.0).astype(BF16)
    put = jnp.concatenate([put_moe, put_grad], axis=0)
    split = count - len(chunks[-1])
    for first, last in ((0, split), (split, count)):
        for k in range(first, last):
            if k != own:
                back[k].wait_recv()
        came = ret[first:last].reshape((last - first) * rows, width)
        placed = jnp.dot(put[:, first * rows:last * rows], came, preferred_element_type=F32)
        if first == 0:
            moe_out[...] = placed[:tokens_here].astype(BF16)
            grad_out[...] = placed[tokens_here:].astype(BF16)
        else:
            moe_out[...] = (moe_out[...].astype(F32) + placed[:tokens_here]).astype(BF16)
            grad_out[...] = (grad_out[...].astype(F32) + placed[tokens_here:]).astype(BF16)

    for k, slot in enumerate(slots):
        if k != own:
            from_dp, from_exp = peer(slot, -1)
            source = from_dp * n_exp + from_exp
            pltpu.make_async_remote_copy(
                src_ref=summed, dst_ref=columns.at[source],
                send_sem=col_send.at[k], recv_sem=col_recv.at[source],
                device_id=at(peer(slot, -1)), device_id_type=MESH,
            ).wait_recv()
    rg_out[...] = columns[...]
    for k in range(count):
        if k != own:
            fwd[k].wait_send()
            back[k].wait_send()
    for copy in ctx_copies + col_copies:
        copy.wait_send()


def per_device(n_dp, n_ctx, n_exp, tokens, cotangent, expert_ids, router_weight, gate_up, down_weight):
    tok_count, width = tokens.shape
    experts = router_weight.shape[1]
    hidden_units = down_weight.shape[1]
    most = min(tok_count, 3 * tok_count * expert_ids.shape[1] // (2 * experts))
    cap = -(-most // 8) * 8
    count = n_dp * n_exp
    rows = 2 * cap
    total = tok_count * n_dp * n_ctx * n_exp
    lines = width // 128
    vmem = pl.BlockSpec(memory_space=pltpu.VMEM)
    hbm = pl.BlockSpec(memory_space=pl.ANY)
    dma = pltpu.SemaphoreType.DMA
    flops = 2 * 2 * count * cap * width * 3 * hidden_units
    moe, grad, columns = pl.pallas_call(
        functools.partial(kernel, n_dp, n_ctx, n_exp, cap, total),
        out_shape=(
            jax.ShapeDtypeStruct((tok_count, width), BF16),
            jax.ShapeDtypeStruct((tok_count, width), BF16),
            jax.ShapeDtypeStruct((experts, lines, 128), F32),
        ),
        in_specs=[vmem, vmem, vmem, vmem, hbm, hbm],
        out_specs=(vmem, vmem, vmem),
        scratch_shapes=[
            pltpu.VMEM((count, rows, width), BF16),
            pltpu.VMEM((count, rows, width), BF16),
            pltpu.VMEM((count, rows, width), BF16),
            pltpu.VMEM((count, rows, width), BF16),
            pltpu.VMEM((width, 2 * hidden_units), BF16),
            pltpu.VMEM((hidden_units, width), BF16),
            pltpu.VMEM((lines, 128), F32),
            pltpu.VMEM((lines, 128), F32),
            pltpu.VMEM((n_ctx, lines, 128), F32),
            pltpu.VMEM((experts, lines, 128), F32),
            dma((2,)),
            dma((count,)),
            dma((count,)),
            dma((count,)),
            dma((count,)),
            dma((n_ctx,)),
            dma((n_ctx,)),
            dma((count,)),
            dma((count,)),
        ],
        compiler_params=pltpu.CompilerParams(
            collective_id=0, has_side_effects=True, vmem_limit_bytes=58 * 1024 * 1024
        ),
        cost_estimate=pl.CostEstimate(
            flops=flops, bytes_accessed=12 * 1024 * 1024, transcendentals=0
        ),
    )(tokens, cotangent, expert_ids, router_weight, gate_up, down_weight)
    return moe, grad, columns.reshape(experts, width).T


def solution(mesh):
    in_specs = (
        P(("dp", "ctx", "exp"), None),
        P(("dp", "ctx", "exp"), None),
        P(("dp", "ctx", "exp"), None),
        P(),
        P(("dp", "exp"), None, None),
        P(("dp", "exp"), None, None),
    )
    out_specs = (P(("dp", "ctx", "exp"), None), P(("dp", "ctx", "exp"), None), P())
    shape = mesh.shape
    return jax.shard_map(
        functools.partial(per_device, shape["dp"], shape["ctx"], shape["exp"]),
        mesh=mesh, in_specs=in_specs, out_specs=out_specs, check_vma=False,
    )
```

```python
import functools

import jax
import jax.numpy as jnp
from jax import lax
from jax.experimental import pallas as pl
from jax.experimental.pallas import tpu as pltpu
from jax.sharding import PartitionSpec as P

MESH = pl.DeviceIdType.MESH
F32 = jnp.float32
BF16 = jnp.bfloat16
NT = (((1,), (1,)), ((), ()))


def plan(n_dp, n_exp):
    half = n_exp // 2
    cut = (half + 1) // 2
    far_a = [(d, 1, o) for o in range(cut) for d in range(n_dp)]
    near = [(d, 0, o) for o in range(half) for d in range(n_dp)]
    far_b = [(d, 1, o) for o in range(cut, half) for d in range(n_dp)]
    return [chunk for chunk in (far_a, near, far_b) if chunk]


def kernel(n_dp, n_ctx, n_exp, cap, total, tok, cot, ids, rw, gu_hbm, dn_hbm,
           moe_out, grad_out, rg_out,
           send, recv, res, ret, gu, dn, mine, summed, terms, columns,
           w_sem, fwd_send, fwd_recv, ret_send, ret_recv,
           ctx_send, ctx_recv, col_send, col_recv):
    me_dp, me_ctx, me_exp = lax.axis_index("dp"), lax.axis_index("ctx"), lax.axis_index("exp")
    me = me_dp * n_exp + me_exp
    half = n_exp // 2
    chunks = plan(n_dp, n_exp)
    slots = [slot for chunk in chunks for slot in chunk]
    count = len(slots)
    own = slots.index((0, 0, 0))
    tokens_here, width = tok.shape
    hidden_units = dn.shape[0]
    experts = rw.shape[0]
    rows = 2 * cap

    def peer(slot, way):
        d, h, o = slot
        if way < 0:
            d, h, o = (n_dp - d) % n_dp, h, (half - o) % half
        to_dp = lax.rem(me_dp + d, n_dp)
        to_half = lax.rem(me_exp // half + h, 2)
        to_low = lax.rem(lax.rem(me_exp, half) + o, half)
        return to_dp, to_half * half + to_low

    def at(pair):
        return {"dp": pair[0], "ctx": me_ctx, "exp": pair[1]}

    def at_ctx(j):
        return {"dp": me_dp, "ctx": j, "exp": me_exp}

    gu_copy = pltpu.make_async_copy(gu_hbm.at[0], gu, w_sem.at[0])
    dn_copy = pltpu.make_async_copy(dn_hbm.at[0], dn, w_sem.at[1])
    gu_copy.start()
    dn_copy.start()

    barrier = pltpu.get_barrier_semaphore()
    for k, slot in enumerate(slots):
        if k != own:
            pl.semaphore_signal(barrier, inc=1, device_id=at(peer(slot, 1)), device_id_type=MESH)
    for j in range(1, n_ctx):
        pl.semaphore_signal(
            barrier, inc=1, device_id=at_ctx(lax.rem(me_ctx + j, n_ctx)), device_id_type=MESH
        )

    ids_row = ids[...]
    r_iota = lax.broadcasted_iota(jnp.int32, (tokens_here, tokens_here), 0)
    c_iota = lax.broadcasted_iota(jnp.int32, (tokens_here, tokens_here), 1)
    ids_wide = jnp.broadcast_to(ids_row, (tokens_here, tokens_here))
    ids_col = jnp.sum(jnp.where(r_iota == c_iota, ids_wide, 0), axis=1, keepdims=True)
    same = ids_col == ids_row
    place_row = jnp.sum(jnp.where(same & (r_iota < c_iota), 1, 0), axis=0, keepdims=True)
    place_col = jnp.sum(jnp.where(same & (c_iota < r_iota), 1, 0), axis=1, keepdims=True)
    for k, slot in enumerate(slots):
        to_dp, to_exp = peer(slot, 1)
        expert = to_dp * n_exp + to_exp
        place_row = place_row + jnp.where(ids_row == expert, k * rows, 0)
        place_col = place_col + jnp.where(ids_col == expert, k * rows, 0)

    pick_iota = lax.broadcasted_iota(jnp.int32, (count * rows, tokens_here), 0)
    pick_tok = jnp.where(pick_iota == place_row, 1.0, 0.0).astype(BF16)
    pick_cot = jnp.where(pick_iota == place_row + cap, 1.0, 0.0).astype(BF16)
    pick = jnp.concatenate([pick_tok, pick_cot], axis=1)
    stacked = jnp.concatenate([tok[...], cot[...]], axis=0)

    fwd = []
    back = []
    for k, slot in enumerate(slots):
        if k == own:
            fwd.append(None)
            back.append(None)
            continue
        fwd.append(
            pltpu.make_async_remote_copy(
                src_ref=send.at[k], dst_ref=recv.at[k],
                send_sem=fwd_send.at[k], recv_sem=fwd_recv.at[k],
                device_id=at(peer(slot, 1)), device_id_type=MESH,
            )
        )
        back.append(
            pltpu.make_async_remote_copy(
                src_ref=res.at[k], dst_ref=ret.at[k],
                send_sem=ret_send.at[k], recv_sem=ret_recv.at[k],
                device_id=at(peer(slot, -1)), device_id_type=MESH,
            )
        )

    starts = [sum(len(c) for c in chunks[:i]) for i in range(len(chunks))]
    order = sorted(range(len(chunks)), key=lambda i: chunks[i][0][1] == 0)
    for number, which in enumerate(order):
        chunk, first = chunks[which], starts[which]
        last = first + len(chunk)
        packed = jnp.dot(
            pick[first * rows:last * rows], stacked, preferred_element_type=F32
        ).astype(BF16)
        send[first:last] = packed.reshape(len(chunk), rows, width)
        if number == 0:
            pl.semaphore_wait(barrier, count - 1 + n_ctx - 1)
        for k in range(first, last):
            if k != own:
                fwd[k].start()

    row_e = lax.broadcasted_iota(jnp.int32, (experts, width), 0)
    router_row = jnp.sum(jnp.where(row_e == me, rw[...].astype(F32), 0.0), axis=0, keepdims=True)

    gu_copy.wait()
    dn_copy.wait()

    router_sum = jnp.zeros((1, width), F32)
    first = 0
    for chunk in chunks:
        last = first + len(chunk)
        xs, cs = [], []
        for k in range(first, last):
            if k == own:
                block = send[k].astype(F32)
            else:
                fwd[k].wait_recv()
                block = recv[k].astype(F32)
            xs.append(block[:cap])
            cs.append(block[cap:])
        x_wide = jnp.concatenate(xs, axis=0)
        c_wide = jnp.concatenate(cs, axis=0)
        m = x_wide.shape[0]
        x = x_wide.astype(BF16)
        logits = lax.dot_general(x, rw[...], NT, preferred_element_type=F32)
        lane = lax.broadcasted_iota(jnp.int32, (m, experts), 1)
        gate = jax.nn.sigmoid(jnp.sum(jnp.where(lane == me, logits, 0.0), axis=1, keepdims=True))
        upstream = (gate * c_wide).astype(BF16)
        pre = jnp.dot(x, gu[...], preferred_element_type=F32)
        a = pre[:, :hidden_units]
        u = pre[:, hidden_units:]
        s = jax.nn.sigmoid(a)
        act = a * s
        hidden = (act * u).astype(BF16)
        out = jnp.dot(hidden, dn[...], preferred_element_type=F32).astype(BF16).astype(F32)
        back_hidden = lax.dot_general(upstream, dn[...], NT, preferred_element_type=F32)
        back_pre = jnp.concatenate(
            [back_hidden * u * (s * (1.0 + a * (1.0 - s))), back_hidden * act], axis=1
        ).astype(BF16)
        back_in = lax.dot_general(back_pre, gu[...], NT, preferred_element_type=F32)
        agreement = jnp.sum(c_wide * out, axis=1, keepdims=True)
        dense = (gate * (1.0 - gate) * agreement).astype(BF16).astype(F32)
        moe = gate * out
        grad = back_in.astype(BF16).astype(F32) + dense * router_row
        for i, k in enumerate(range(first, last)):
            part = slice(i * cap, (i + 1) * cap)
            block = jnp.concatenate([moe[part], grad[part]], axis=0).astype(BF16)
            if k == own:
                ret[k] = block
            else:
                res[k] = block
                back[k].start()
        router_sum = router_sum + jnp.sum(dense * x_wide, axis=0, keepdims=True)
        first = last

    router_sum = router_sum * (1.0 / total)
    lanes = width // mine.shape[0]
    for i in range(mine.shape[0]):
        mine[i:i + 1, :] = router_sum[:, i * lanes:(i + 1) * lanes]
    terms[me_ctx] = mine[...]
    ctx_copies = []
    for j in range(1, n_ctx):
        copy = pltpu.make_async_remote_copy(
            src_ref=mine, dst_ref=terms.at[me_ctx],
            send_sem=ctx_send.at[j], recv_sem=ctx_recv.at[me_ctx],
            device_id=at_ctx(lax.rem(me_ctx + j, n_ctx)), device_id_type=MESH,
        )
        copy.start()
        ctx_copies.append(copy)
    for j in range(1, n_ctx):
        source = lax.rem(me_ctx + j, n_ctx)
        pltpu.make_async_remote_copy(
            src_ref=mine, dst_ref=terms.at[source],
            send_sem=ctx_send.at[j], recv_sem=ctx_recv.at[source],
            device_id=at_ctx(source), device_id_type=MESH,
        ).wait_recv()
    column = terms[0]
    for j in range(1, n_ctx):
        column = column + terms[j]
    summed[...] = column
    columns[me] = column
    col_copies = []
    for k, slot in enumerate(slots):
        if k != own:
            copy = pltpu.make_async_remote_copy(
                src_ref=summed, dst_ref=columns.at[me],
                send_sem=col_send.at[k], recv_sem=col_recv.at[me],
                device_id=at(peer(slot, 1)), device_id_type=MESH,
            )
            copy.start()
            col_copies.append(copy)

    spot_iota = lax.broadcasted_iota(jnp.int32, (tokens_here, count * rows), 1)
    put_moe = jnp.where(spot_iota == place_col, 1.0, 0.0).astype(BF16)
    put_grad = jnp.where(spot_iota == place_col + cap, 1.0, 0.0).astype(BF16)
    put = jnp.concatenate([put_moe, put_grad], axis=0)
    split = count - len(chunks[-1])
    for first, last in ((0, split), (split, count)):
        for k in range(first, last):
            if k != own:
                back[k].wait_recv()
        came = ret[first:last].reshape((last - first) * rows, width)
        placed = jnp.dot(put[:, first * rows:last * rows], came, preferred_element_type=F32)
        if first == 0:
            moe_out[...] = placed[:tokens_here].astype(BF16)
            grad_out[...] = placed[tokens_here:].astype(BF16)
        else:
            moe_out[...] = (moe_out[...].astype(F32) + placed[:tokens_here]).astype(BF16)
            grad_out[...] = (grad_out[...].astype(F32) + placed[tokens_here:]).astype(BF16)

    for k, slot in enumerate(slots):
        if k != own:
            from_dp, from_exp = peer(slot, -1)
            source = from_dp * n_exp + from_exp
            pltpu.make_async_remote_copy(
                src_ref=summed, dst_ref=columns.at[source],
                send_sem=col_send.at[k], recv_sem=col_recv.at[source],
                device_id=at(peer(slot, -1)), device_id_type=MESH,
            ).wait_recv()
    for i in range(mine.shape[0]):
        rg_out[:, i * lanes:(i + 1) * lanes] = columns[:, i, :]
    for k in range(count):
        if k != own:
            fwd[k].wait_send()
            back[k].wait_send()
    for copy in ctx_copies + col_copies:
        copy.wait_send()


def hand_over(moe, grad, columns, moe_out, grad_out, rg_out, moe_buf, grad_buf, rg_buf, in_sem, out_sem):
    half = moe.shape[0] // 2
    parts = [(columns, rg_buf, rg_out)]
    for source, buffer, target in ((moe, moe_buf, moe_out), (grad, grad_buf, grad_out)):
        for start in (0, half):
            cut = pl.ds(start, half)
            parts.append((source.at[cut], buffer.at[cut], target.at[cut]))
    loads, stores = [], []
    for i, (source, buffer, target) in enumerate(parts):
        loads.append(pltpu.make_async_copy(source, buffer, in_sem.at[i]))
        stores.append(pltpu.make_async_copy(buffer, target, out_sem.at[i]))
    for load in loads:
        load.start()
    for load, store in zip(loads, stores):
        load.wait()
        store.start()
    for store in stores:
        store.wait()


def per_device(n_dp, n_ctx, n_exp, tokens, cotangent, expert_ids, router_weight, gate_up, down_weight):
    tok_count, width = tokens.shape
    experts = router_weight.shape[1]
    hidden_units = down_weight.shape[1]
    most = min(tok_count, 3 * tok_count * expert_ids.shape[1] // (2 * experts))
    cap = -(-most // 8) * 8
    count = n_dp * n_exp
    rows = 2 * cap
    total = tok_count * n_dp * n_ctx * n_exp
    lines = width // 128
    vmem = pl.BlockSpec(memory_space=pltpu.VMEM)
    hbm = pl.BlockSpec(memory_space=pl.ANY)
    dma = pltpu.SemaphoreType.DMA
    flops = 2 * 2 * count * cap * width * 3 * hidden_units
    moe, grad, columns = pl.pallas_call(
        functools.partial(kernel, n_dp, n_ctx, n_exp, cap, total),
        out_shape=(
            jax.ShapeDtypeStruct((tok_count, width), BF16),
            jax.ShapeDtypeStruct((tok_count, width), BF16),
            jax.ShapeDtypeStruct((experts, width), F32),
        ),
        in_specs=[vmem, vmem, vmem, vmem, hbm, hbm],
        out_specs=(vmem, vmem, vmem),
        scratch_shapes=[
            pltpu.VMEM((count, rows, width), BF16),
            pltpu.VMEM((count, rows, width), BF16),
            pltpu.VMEM((count, rows, width), BF16),
            pltpu.VMEM((count, rows, width), BF16),
            pltpu.VMEM((width, 2 * hidden_units), BF16),
            pltpu.VMEM((hidden_units, width), BF16),
            pltpu.VMEM((lines, 128), F32),
            pltpu.VMEM((lines, 128), F32),
            pltpu.VMEM((n_ctx, lines, 128), F32),
            pltpu.VMEM((experts, lines, 128), F32),
            dma((2,)),
            dma((count,)),
            dma((count,)),
            dma((count,)),
            dma((count,)),
            dma((n_ctx,)),
            dma((n_ctx,)),
            dma((count,)),
            dma((count,)),
        ],
        compiler_params=pltpu.CompilerParams(
            collective_id=0, has_side_effects=True, vmem_limit_bytes=58 * 1024 * 1024
        ),
        cost_estimate=pl.CostEstimate(
            flops=flops, bytes_accessed=12 * 1024 * 1024, transcendentals=0
        ),
    )(tokens, cotangent, expert_ids.reshape(1, tok_count), router_weight.T, gate_up, down_weight)
    moe, grad, columns = pl.pallas_call(
        hand_over,
        out_shape=tuple(jax.ShapeDtypeStruct(v.shape, v.dtype) for v in (moe, grad, columns)),
        in_specs=[hbm, hbm, hbm],
        out_specs=(hbm, hbm, hbm),
        scratch_shapes=[
            pltpu.VMEM(moe.shape, BF16),
            pltpu.VMEM(grad.shape, BF16),
            pltpu.VMEM(columns.shape, F32),
            dma((5,)),
            dma((5,)),
        ],
    )(moe, grad, columns)
    return moe, grad, columns.T


def solution(mesh):
    in_specs = (
        P(("dp", "ctx", "exp"), None),
        P(("dp", "ctx", "exp"), None),
        P(("dp", "ctx", "exp"), None),
        P(),
        P(("dp", "exp"), None, None),
        P(("dp", "exp"), None, None),
    )
    out_specs = (P(("dp", "ctx", "exp"), None), P(("dp", "ctx", "exp"), None), P())
    shape = mesh.shape
    return jax.shard_map(
        functools.partial(per_device, shape["dp"], shape["ctx"], shape["exp"]),
        mesh=mesh, in_specs=in_specs, out_specs=out_specs, check_vma=False,
    )
```
